32 devices in a mesh: passage: 2 (over x), brick: 16 (over z, y, core).
Axes of the slice: x: 2, y: 2, z: 4, core: 2. Of those that a mesh axis runs over, the one named last changes fastest.
Arguments:
- jac_blocks: bfloat16 [2, 25, 16, 8192], P('passage', None, None, 'brick'), may hold values from -6 to 6
- psi_start: float32 [2, 10, 16, 64, 128], P('passage', None, 'brick'), may hold values from -6 to 6
- source: float32 [2, 10, 16, 64, 128], P('passage', None, 'brick'), may hold values from -6 to 6
- pseudo_step: float32 [2, 16, 64, 128], P('passage', 'brick'), may hold values from 0.1 to 0.4
- dissipation: float32 [2, 16, 64, 128], P('passage', 'brick'), may hold values from 0.04 to 0.15
- freq_volume: float32 [2, 16, 64, 128], P('passage', 'brick'), may hold values from 0.2 to 2
- normals: float32 [2, 3, 16, 64], P('passage', None, 'brick'), may hold values from -6 to 6
- face_owner: int32 [2, 1024, 1], P('passage', 'brick'), may hold values from 0 to 15; in each aligned block of 64 rows (0 to 63, 64 to 127, ..., all dimensions but the last counted through in order) at most 16 rows name the same one
- face_slot: int32 [2, 1024], P('passage', 'brick'), may hold values from 0 to 255
Outputs:
- adjoint: float32 [2, 10, 16, 64, 128], P('passage', None, 'brick')
- sensitivity: float32 [2, 6, 4096], P('passage', None, 'brick')
The draws below stay inside these ranges and needn't reach their ends.
Inputs may be any that keep to these rules, and one draw needn't show every extreme that they name: `face_owner`: in the 64 faces of one device (aligned blocks of the rows), no brick is named by more than 16 faces, and in some block some brick is named by exactly 16.
All inputs are finite; a program needn't handle non-finite values.
Results may differ from the reference program's by a relative error of at most 0.0003.
Values may be sent and summed in bfloat16 or wider, within the bound.
A program may use at most 64 MiB of HBM per device.

```python
import math
import jax
import jax.numpy as jnp
import numpy as np

PASSAGES = 2
CI = 1
NJ = 64
NK = 128
NI = 16
NJK = 8192
NODE_DEV = 256
NODES = 4096
CAP = 16
SWEEPS = 2
ND = 1
BLADES = 36
N_BRICK = 16


def plant(array, stream_key, least, largest):
    dims = array.shape
    spot = [jax.random.randint(jax.random.fold_in(stream_key, axis), (), 0, dims[axis]) for axis in range(len(dims))]
    array = array.at[tuple(spot)].set(least)
    longest = dims.index(max(dims))
    spot[longest] = (spot[longest] + 1) % dims[longest]
    return array.at[tuple(spot)].set(largest)


def block_levels(own_key, extent, shards, smallest, largest):
    def one(axis_at, blocks):
        steps = jax.random.uniform(jax.random.fold_in(jax.random.fold_in(own_key, 6), axis_at), (blocks,), jnp.float32, smallest / len(shards), largest / len(shards))
        return jnp.repeat(jnp.exp(steps), extent[axis_at] // blocks).reshape((-1,) + (1,) * (len(extent) - axis_at - 1))

    level = one(*shards[0])
    for cut in shards[1:]:
        level = level * one(*cut)
    return level


def routed_block(key, own, number, rows, number_of, top, most, slope):
    sequence = jax.random.permutation(key, number_of)
    crowded, ordinary = shares(number_of, rows * top, most, slope, True), shares(number_of, rows * top, most, slope, False)
    places = jnp.arange(number_of)

    def named(sizes, turn):
        used = int((sizes > 0).sum())
        fixed = max(1, used // 4)
        shifted = fixed + (places - fixed + turn * (used - fixed)) % max(1, number_of - fixed)
        return jnp.zeros((number_of,), jnp.int32).at[sequence[jnp.where(places < fixed, places, shifted)]].set(jnp.asarray(sizes, jnp.int32))

    sizes = jnp.where(number % 4 == 0, named(crowded, number // 4), named(ordinary, number - number // 4 - 1))
    mixed = jax.random.permutation(jax.random.fold_in(own, 3), number_of)
    donor, sink = mixed[0:number_of // 2 * 2:2], mixed[1:number_of // 2 * 2:2]
    slack = jnp.minimum(sizes[donor] - 1, most - sizes[sink]) // 2
    slack = jnp.where((donor == sequence[0]) | (sink == sequence[0]) | (sizes[sink] == 0), 0, jnp.maximum(slack, 0))
    shifted = jax.random.randint(jax.random.fold_in(own, 4), (number_of // 2,), 0, 1 << 20) % (slack + 1)
    sizes = sizes.at[donor].add(-shifted).at[sink].add(shifted)
    members = jnp.searchsorted(jnp.cumsum(sizes), jnp.arange(rows * top), side="right").astype(jnp.int32)
    table = members.reshape(top, rows).T
    table = table[jax.random.permutation(jax.random.fold_in(own, 1), rows)]
    turn = jax.random.randint(jax.random.fold_in(own, 2), (rows, 1), 0, top)
    return jnp.take_along_axis(table, (jnp.arange(top)[None, :] + turn) % top, axis=1)


def shares(count, total, most, skew, full):
    loads = [(1 << 20) // math.isqrt(rank ** skew) + 1 for rank in range(1, count + 1)]
    largest = most if full else min(most, max(-(-total // count), total * loads[0] // sum(loads)))
    least = 1 if total - largest >= count - 1 else 0
    counts, rest = [largest] + [least] * (count - 1), total - largest - least * (count - 1)
    while rest > 0:
        candidates = [i for i in range(1, count) if counts[i] < largest] or [i for i in range(1, count) if counts[i] < most]
        mass, budget = sum([loads[i] for i in candidates]), rest
        for i in candidates:
            more = min(most - counts[i], max(1, budget * loads[i] // mass), rest)
            counts[i] = counts[i] + more
            rest = rest - more
    return np.array(counts)


def noise(key, shape, spread, limit, shards=(), dtype=jnp.bfloat16):
    values = spread * jax.random.normal(key, shape, jnp.float32)
    if shards:
        values = values * block_levels(key, shape, shards, -0.22, 0.18)
    return jnp.clip(values, -limit, limit).astype(dtype)


def setup_inputs(seed: int = 0) -> dict:
    seeds = jax.random.split(jax.random.key(seed), 10)
    jac_blocks = noise(seeds[0], (PASSAGES, 25, NI, NJK), 0.4, 6.0, ((0, 2), (3, 16)))
    psi_start = noise(seeds[1], (PASSAGES, 10, NI, NJ, NK), 1.0, 6.0, ((0, 2), (2, 16)), jnp.float32)
    source = noise(seeds[2], (PASSAGES, 10, NI, NJ, NK), 1.0, 6.0, ((0, 2), (2, 16)), jnp.float32)
    pseudo_step = jnp.clip(jnp.exp(math.log(0.4) - 1.3862944 * jax.random.uniform(seeds[3], (PASSAGES, NI, NJ, NK), jnp.float32) ** block_levels(seeds[3], (PASSAGES, NI, NJ, NK), ((0, 2), (1, 16)), -0.2, 0.2)), 0.1, 0.4)
    dissipation = jnp.clip(jnp.exp(math.log(0.15) - 1.3217559 * jax.random.uniform(seeds[4], (PASSAGES, NI, NJ, NK), jnp.float32) ** block_levels(seeds[4], (PASSAGES, NI, NJ, NK), ((0, 2), (1, 16)), -0.2, 0.2)), 0.04, 0.15)
    freq_volume = jnp.clip(jnp.exp(math.log(2.0) - 2.3025851 * jax.random.uniform(seeds[5], (PASSAGES, NI, NJ, NK), jnp.float32) ** block_levels(seeds[5], (PASSAGES, NI, NJ, NK), ((0, 2), (1, 16)), -0.2, 0.2)), 0.2, 2.0)
    normals = noise(seeds[6], (PASSAGES, 3, NI, NJ), 1.0, 6.0, ((0, 2), (2, 16)), jnp.float32)
    face_owner_keys = jax.random.split(jax.random.fold_in(seeds[7], 1), PASSAGES * (NI * NJ) // (CI * NJ))
    face_owner_turns = jax.random.permutation(jax.random.fold_in(seeds[7], 3), PASSAGES * (NI * NJ) // (CI * NJ))
    face_owner = jax.vmap(lambda own, number: routed_block(jax.random.fold_in(seeds[7], 2), own, number, CI * NJ, N_BRICK, 1, CAP, 2))(face_owner_keys, face_owner_turns).reshape((PASSAGES, NI * NJ, 1))
    face_slot = plant(jax.random.randint(seeds[8], (PASSAGES, NI * NJ), 0, NODE_DEV), jax.random.fold_in(seeds[8], 1), 0, NODE_DEV - 1).astype(jnp.int32)
    return dict(jac_blocks=jac_blocks, psi_start=psi_start, source=source, pseudo_step=pseudo_step, dissipation=dissipation, freq_volume=freq_volume, normals=normals, face_owner=face_owner, face_slot=face_slot)


def rotate(rim, turn):
    cosine = math.cos(turn)
    sine = math.sin(turn)
    real_part = rim[:, :5]
    imag_part = rim[:, 5:]
    return jnp.concatenate([real_part * cosine - imag_part * sine, real_part * sine + imag_part * cosine], axis=1)


def transpose_apply(tiles, diff):
    total_real = jnp.zeros_like(diff[:, :5])
    total_imag = jnp.zeros_like(diff[:, :5])
    for row_index in range(5):
        column = tiles[:, row_index * 5:row_index * 5 + 5].astype(jnp.float32)
        total_real = total_real + column * diff[:, row_index:row_index + 1]
        total_imag = total_imag + column * diff[:, 5 + row_index:6 + row_index]
    return jnp.concatenate([total_real, total_imag], axis=1)


def reference(jac_blocks, psi_start, source, pseudo_step, dissipation, freq_volume, normals, face_owner, face_slot):
    passes = psi_start.shape[0]
    phase_angle = 2.0 * math.pi * ND * passes / BLADES
    tiles = jac_blocks.reshape(passes, 25, NI, NJ, NK)
    cycle_index = jnp.arange(passes).reshape(passes, 1, 1, 1, 1)
    state = psi_start
    for sweep in range(SWEEPS):
        below_rim = jnp.roll(state[:, :, :, -1:], 1, axis=0)
        below_rim = jnp.where(cycle_index == 0, rotate(below_rim, -phase_angle), below_rim)
        above_rim = jnp.roll(state[:, :, :, :1], -1, axis=0)
        above_rim = jnp.where(cycle_index == passes - 1, rotate(above_rim, phase_angle), above_rim)
        padded_j = jnp.concatenate([below_rim, state, above_rim], axis=3)
        padded_i = jnp.pad(state, ((0, 0), (0, 0), (1, 1), (0, 0), (0, 0)))
        padded_k = jnp.pad(state, ((0, 0), (0, 0), (0, 0), (0, 0), (1, 1)))
        beside = padded_i[:, :, 2:] + padded_i[:, :, :-2]
        beside = beside + padded_j[:, :, :, 2:] + padded_j[:, :, :, :-2]
        beside = beside + padded_k[..., 2:] + padded_k[..., :-2]
        diff = 0.5 * (padded_i[:, :, 2:] - padded_i[:, :, :-2])
        convect = transpose_apply(tiles, diff)
        omega = freq_volume[:, None]
        spin = jnp.concatenate([omega * state[:, 5:], -omega * state[:, :5]], axis=1)
        resid = convect + spin + dissipation[:, None] * (6.0 * state - beside) - source
        state = state - pseudo_step[:, None] * resid
    wall_state = state[..., 0]
    values = jnp.concatenate([normals * wall_state[:, 1:4], normals * wall_state[:, 6:9]], axis=1)
    values = values.reshape(passes, 6, NI * NJ)
    node_ids = (face_owner[..., 0] * NODE_DEV + face_slot).astype(jnp.int32)
    results = []
    for part_index in range(passes):
        summed = jnp.zeros((6, NODES), jnp.float32).at[:, node_ids[part_index]].add(values[part_index])
        results.append(summed)
    return state, jnp.stack(results, axis=0)
```

```python
import functools
import math

import jax
import jax.numpy as jnp
from jax import lax
from jax.experimental import pallas as pl
from jax.experimental.pallas import tpu as pltpu
from jax.sharding import PartitionSpec as P

NODE_DEV = 256
SWEEPS = 2
ND = 1
BLADES = 36
LANES = 128
SUB = 8
MESH = pl.DeviceIdType.MESH


def far_first(count):
    half = count // 2
    return sorted(range(1, count), key=lambda d: (abs(d - half), d))


def kernel(
    B, passes, phase_angle,
    jac, psi, source, pstep, diss, freq, normals, ids,
    adj, sens,
    jpack, jsend, jrecv, jflat, pad0, pad1, low0, high0, low1, high1,
    rim_send, rim_recv, idbuf, valbuf,
    j_s, j_r, h_s, h_r, r_s, r_r, i_s, i_r, v_s, v_r,
):
    me = lax.axis_index("brick")
    mp = lax.axis_index("passage")
    NJ, NK = psi.shape[1], psi.shape[2]
    R = jac.shape[2] // LANES
    planes = jac.shape[1]
    rows = 25 * R
    pitch = jpack.shape[0] // planes
    others = far_first(B)
    up_p = lax.rem(mp + 1, passes)
    down_p = lax.rem(mp + passes - 1, passes)

    barrier = pltpu.get_barrier_semaphore()
    for d in others:
        pl.semaphore_signal(
            barrier, inc=1, device_id={"brick": lax.rem(me + d, B)}, device_id_type=MESH
        )
    pl.semaphore_signal(barrier, inc=1, device_id={"passage": up_p}, device_id_type=MESH)
    greeted = B
    if passes > 2:
        pl.semaphore_signal(barrier, inc=1, device_id={"passage": down_p}, device_id_type=MESH)
        greeted += 1

    for n in range(25):
        for r in range(R):
            for g in range(planes // SUB):
                x = jac[n, pl.ds(g * SUB, SUB), pl.ds(r * LANES, LANES)].astype(jnp.float32)
                jpack[pl.ds(g * SUB * pitch + r * 25 + n, SUB, stride=pitch), :] = x
    for p in range(planes):
        jsend[p, :, :] = jpack[pl.ds(p * pitch, rows), :].astype(jnp.bfloat16)

    def fill_rims(sweep, field, first, last):
        for c in range(10):
            rim_send[sweep, 0, pl.ds(c, 1), :] = field[c, pl.ds(last, 1), :]
            rim_send[sweep, 1, pl.ds(c, 1), :] = field[c, pl.ds(first, 1), :]

    def rim_copies(sweep):
        return [
            pltpu.make_async_remote_copy(
                src_ref=rim_send.at[sweep, k],
                dst_ref=rim_recv.at[sweep, k],
                send_sem=r_s.at[sweep, k],
                recv_sem=r_r.at[sweep, k],
                device_id={"passage": peer},
                device_id_type=MESH,
            )
            for k, peer in ((0, up_p), (1, down_p))
        ]

    def halo_copies(sweep, src, low, high):
        up = pltpu.make_async_remote_copy(
            src_ref=src, dst_ref=low, send_sem=h_s.at[sweep, 0], recv_sem=h_r.at[sweep, 0],
            device_id={"brick": lax.rem(me + 1, B)}, device_id_type=MESH,
        )
        down = pltpu.make_async_remote_copy(
            src_ref=src, dst_ref=high, send_sem=h_s.at[sweep, 1], recv_sem=h_r.at[sweep, 1],
            device_id={"brick": lax.rem(me + B - 1, B)}, device_id_type=MESH,
        )
        return up, down

    def halo_start(up, down):
        @pl.when(me < B - 1)
        def _():
            up.start()

        @pl.when(me > 0)
        def _():
            down.start()

    def halo_recv(up, down, low, high):
        @pl.when(me > 0)
        def _():
            up.wait_recv()

        @pl.when(me == 0)
        def _():
            low[...] = jnp.zeros_like(low)

        @pl.when(me < B - 1)
        def _():
            down.wait_recv()

        @pl.when(me == B - 1)
        def _():
            high[...] = jnp.zeros_like(high)

    def halo_sent(up, down):
        @pl.when(me < B - 1)
        def _():
            up.wait_send()

        @pl.when(me > 0)
        def _():
            down.wait_send()

    fill_rims(0, psi, 0, NJ - 1)
    idbuf[pl.ds(me, 1), :, :] = ids[...].reshape(1, SUB, LANES)

    j_copies, id_copies, val_copies = [], [], []
    for k, d in enumerate(others):
        peer = lax.rem(me + d, B)
        j_copies.append(pltpu.make_async_remote_copy(
            src_ref=jsend.at[peer], dst_ref=jrecv.at[me], send_sem=j_s.at[k], recv_sem=j_r.at[k],
            device_id={"brick": peer}, device_id_type=MESH))
        id_copies.append(pltpu.make_async_remote_copy(
            src_ref=ids, dst_ref=idbuf.at[me], send_sem=i_s.at[k], recv_sem=i_r.at[k],
            device_id={"brick": peer}, device_id_type=MESH))
        val_copies.append(pltpu.make_async_remote_copy(
            src_ref=valbuf.at[me], dst_ref=valbuf.at[me], send_sem=v_s.at[k], recv_sem=v_r.at[k],
            device_id={"brick": peer}, device_id_type=MESH))
    rims0, rims1 = rim_copies(0), rim_copies(1)
    halo0 = halo_copies(0, psi, low0, high0)
    inner = pad1.at[:, pl.ds(SUB, NJ), :]
    halo1 = halo_copies(1, inner, low1, high1)

    pl.semaphore_wait(barrier, greeted)
    for copy in j_copies:
        copy.start()
    for copy in rims0:
        copy.start()
    halo_start(*halo0)
    for copy in id_copies:
        copy.start()

    jrecv[pl.ds(me, 1), :, :] = jsend[pl.ds(me, 1), :, :]
    for c in range(10):
        pad0[c, pl.ds(SUB, NJ), :] = psi[c, :, :]

    lane = lax.broadcasted_iota(jnp.int32, (SUB, NK), 1)

    def place_rims(sweep, pad):
        for k, (edge, turn, row) in enumerate(
            ((0, -phase_angle, SUB - 1), (passes - 1, phase_angle, SUB + NJ))
        ):
            rim = rim_recv[sweep, k, :, :]
            re, im = rim[0:5], rim[5:10]
            at_edge = mp == edge
            cosine = jnp.where(at_edge, math.cos(turn), 1.0).astype(jnp.float32)
            sine = jnp.where(at_edge, math.sin(turn), 0.0).astype(jnp.float32)
            re, im = re * cosine - im * sine, re * sine + im * cosine
            for c in range(5):
                pad[c, pl.ds(row, 1), :] = re[c : c + 1]
                pad[5 + c, pl.ds(row, 1), :] = im[c : c + 1]

    def advance(pad, low, high, out, shift):
        for t in range(NJ // SUB):
            at = pl.ds(t * SUB, SUB)
            om, ds_, ps = freq[at, :], diss[at, :], pstep[at, :]
            us, lows, highs = [], [], []
            for c in range(10):
                us.append(pad[c, pl.ds(SUB + t * SUB, SUB), :])
                lows.append(low[c, at, :])
                highs.append(high[c, at, :])
            diff = [0.5 * (h - l) for h, l in zip(highs, lows)]
            conv = [None] * 10
            for n in range(5):
                for m in range(5):
                    tile = jflat[pl.ds(t * SUB * 25 + n * 5 + m, SUB, stride=25), :]
                    for part in (0, 5):
                        term = tile * diff[part + n]
                        conv[part + m] = term if conv[part + m] is None else conv[part + m] + term
            for c in range(10):
                u = us[c]
                beside = highs[c] + lows[c]
                beside = beside + pad[c, pl.ds(SUB + t * SUB + 1, SUB), :]
                beside = beside + pad[c, pl.ds(SUB + t * SUB - 1, SUB), :]
                beside = beside + jnp.where(lane == NK - 1, 0.0, pltpu.roll(u, NK - 1, 1))
                beside = beside + jnp.where(lane == 0, 0.0, pltpu.roll(u, 1, 1))
                spin = om * us[c + 5] if c < 5 else -(om * us[c - 5])
                resid = conv[c] + spin + ds_ * (6.0 * u - beside) - source[c, at, :]
                out[c, pl.ds(shift + t * SUB, SUB), :] = u - ps * resid

    for copy in rims0:
        copy.wait_recv()
    place_rims(0, pad0)
    halo_recv(*halo0, low0, high0)
    for copy in j_copies:
        copy.wait_recv()
    for s in range(B):
        jflat[pl.ds(s * rows, rows), :] = jrecv[s, :, :].astype(jnp.float32)

    advance(pad0, low0, high0, pad1, SUB)
    fill_rims(1, pad1, SUB, SUB + NJ - 1)
    halo_start(*halo1)
    for copy in rims1:
        copy.start()
    for copy in rims1:
        copy.wait_recv()
    place_rims(1, pad1)
    halo_recv(*halo1, low1, high1)
    advance(pad1, low1, high1, adj, 0)

    lanes = lax.broadcasted_iota(jnp.int32, (NJ, NK), 1)
    wall = jnp.zeros((NJ, NK), jnp.float32)
    for k, c in enumerate((1, 2, 3, 6, 7, 8)):
        column = adj[c, :, :]
        if k:
            column = pltpu.roll(column, k, 1)
        wall = jnp.where(lanes == k, column, wall)
    if NJ < LANES:
        wall = jnp.concatenate([wall, jnp.zeros((LANES - NJ, NK), jnp.float32)], axis=0)
    values = wall.T[0:SUB] * normals[...]
    valbuf[pl.ds(me, 1), :, :] = values.reshape(1, SUB, LANES)
    for copy in val_copies:
        copy.start()

    for copy in id_copies:
        copy.wait_recv()
    for copy in val_copies:
        copy.wait_recv()
    node = lax.broadcasted_iota(jnp.int32, (NODE_DEV, LANES), 0) + me * NODE_DEV
    total = jnp.zeros((3 * SUB, NODE_DEV), jnp.float32)
    for s in range(B):
        hit = jnp.where(idbuf[s, 0:1, :] == node, 1.0, 0.0).astype(jnp.bfloat16)
        v = valbuf[s, :, :]
        a = v.astype(jnp.bfloat16).astype(jnp.float32)
        rest = v - a
        b = rest.astype(jnp.bfloat16).astype(jnp.float32)
        parts = jnp.concatenate([a, b, rest - b], axis=0).astype(jnp.bfloat16)
        total = total + lax.dot_general(
            parts, hit, (((1,), (1,)), ((), ())), preferred_element_type=jnp.float32
        )
    summed = total[0:SUB] + total[SUB : 2 * SUB] + total[2 * SUB :]
    sens[...] = summed[0:6]

    for copy in j_copies + id_copies + val_copies + rims0 + rims1:
        copy.wait_send()
    halo_sent(*halo0)
    halo_sent(*halo1)


def body(B, passes, jac_blocks, psi_start, source, pseudo_step, dissipation, freq_volume,
         normals, face_owner, face_slot):
    _, _, planes_all, cells = jac_blocks.shape
    NJ, NK = psi_start.shape[3:]
    phase_angle = 2.0 * math.pi * ND * passes / BLADES
    R = cells // LANES
    rows = 25 * R
    pitch = -(-rows // SUB) * SUB
    node_ids = face_owner[:, :, 0] * NODE_DEV + face_slot
    ids = jnp.pad(node_ids, ((0, SUB - 1), (0, LANES - node_ids.shape[1])), constant_values=-1)
    face_normals = normals[0, :, 0, :]
    face_normals = jnp.concatenate([face_normals, face_normals], axis=0)
    face_normals = jnp.pad(
        face_normals, ((0, SUB - 6), (0, LANES - face_normals.shape[1])))
    f32 = jnp.float32
    field = (10, NJ, NK)
    vm = pl.BlockSpec(memory_space=pltpu.VMEM)
    dma = pltpu.SemaphoreType.DMA
    adj, sens = pl.pallas_call(
        functools.partial(kernel, B, passes, phase_angle),
        out_shape=(
            jax.ShapeDtypeStruct(field, f32),
            jax.ShapeDtypeStruct((6, NODE_DEV), f32),
        ),
        in_specs=[vm] * 8,
        out_specs=(vm, vm),
        scratch_shapes=[
            pltpu.VMEM((planes_all * pitch, LANES), f32),
            pltpu.VMEM((planes_all, rows, LANES), jnp.bfloat16),
            pltpu.VMEM((planes_all, rows, LANES), jnp.bfloat16),
            pltpu.VMEM((B * rows, LANES), f32),
            pltpu.VMEM((10, NJ + 2 * SUB, NK), f32),
            pltpu.VMEM((10, NJ + 2 * SUB, NK), f32),
            pltpu.VMEM(field, f32),
            pltpu.VMEM(field, f32),
            pltpu.VMEM(field, f32),
            pltpu.VMEM(field, f32),
            pltpu.VMEM((2, 2, 2 * SUB, NK), f32),
            pltpu.VMEM((2, 2, 2 * SUB, NK), f32),
            pltpu.VMEM((B, SUB, LANES), jnp.int32),
            pltpu.VMEM((B, SUB, LANES), f32),
            dma((B,)), dma((B,)),
            dma((2, 2)), dma((2, 2)),
            dma((2, 2)), dma((2, 2)),
            dma((B,)), dma((B,)),
            dma((B,)), dma((B,)),
        ],
        compiler_params=pltpu.CompilerParams(collective_id=0, has_side_effects=True),
        name="flutter",
    )(jac_blocks[0], psi_start[0, :, 0], source[0, :, 0], pseudo_step[0, 0], dissipation[0, 0],
      freq_volume[0, 0], face_normals, ids)
    return adj[None, :, None], sens[None]


def solution(mesh):
    placed = (
        P("passage", None, None, "brick"),
        P("passage", None, "brick", None, None),
        P("passage", None, "brick", None, None),
        P("passage", "brick", None, None),
        P("passage", "brick", None, None),
        P("passage", "brick", None, None),
        P("passage", None, "brick", None),
        P("passage", "brick", None),
        P("passage", "brick"),
    )
    return jax.shard_map(
        functools.partial(body, mesh.shape["brick"], mesh.shape["passage"]),
        mesh=mesh,
        in_specs=placed,
        out_specs=(P("passage", None, "brick", None, None), P("passage", None, "brick")),
        check_vma=False,
    )
```

```python
import functools
import math

import jax
import jax.numpy as jnp
from jax import lax
from jax.experimental import pallas as pl
from jax.experimental.pallas import tpu as pltpu
from jax.sharding import PartitionSpec as P

NODE_DEV = 256
SWEEPS = 2
ND = 1
BLADES = 36
LANES = 128
SUB = 8
CODE = 32767.0
BOUND = 6.0
MESH = pl.DeviceIdType.MESH


def far_first(count):
    half = count // 2
    return sorted(range(1, count), key=lambda d: (abs(d - half), d))


def kernel(
    B, passes, phase_angle,
    jac_h, psi_h, source_h, pstep_h, diss_h, freq_h, normals_h, owner_h, slot_h,
    adj_h, sens,
    jac, source, pstep, diss, freq, normals_v, owner, slot, adj, normals, ids,
    jpack, jsend, jrecv, jflat, pad0, pad1, low, high,
    code0, low0, high0, code1, low1, high1, scale1, low_scale, high_scale,
    rim_send, rim_recv, idbuf, valbuf,
    l_s, o_s, j_s, j_r, h_s, h_r, c_s, c_r, r_s, r_r, i_s, i_r, v_s, v_r,
):
    me = lax.axis_index("brick")
    mp = lax.axis_index("passage")
    NJ, NK = source.shape[1], source.shape[2]
    R = jac.shape[2] // LANES
    planes = jac.shape[1]
    rows = 25 * R
    pitch = jpack.shape[0] // planes
    others = far_first(B)
    up_p = lax.rem(mp + 1, passes)
    down_p = lax.rem(mp + passes - 1, passes)

    barrier = pltpu.get_barrier_semaphore()
    for d in others:
        pl.semaphore_signal(
            barrier, inc=1, device_id={"brick": lax.rem(me + d, B)}, device_id_type=MESH
        )
    pl.semaphore_signal(barrier, inc=1, device_id={"passage": up_p}, device_id_type=MESH)
    greeted = B
    if passes > 2:
        pl.semaphore_signal(barrier, inc=1, device_id={"passage": down_p}, device_id_type=MESH)
        greeted += 1

    psi = pad0.at[:, pl.ds(SUB, NJ), :]
    loads = [
        pltpu.make_async_copy(src, dst, l_s.at[k])
        for k, (src, dst) in enumerate((
            (jac_h, jac), (psi_h, psi), (owner_h, owner), (slot_h, slot), (normals_h, normals_v),
            (source_h, source), (pstep_h, pstep), (diss_h, diss), (freq_h, freq),
        ))
    ]
    for load in loads:
        load.start()

    @pl.when(me == 0)
    def _():
        low0[...] = jnp.zeros_like(low0)
        low1[...] = jnp.zeros_like(low1)
        low_scale[...] = jnp.zeros_like(low_scale)

    @pl.when(me == B - 1)
    def _():
        high0[...] = jnp.zeros_like(high0)
        high1[...] = jnp.zeros_like(high1)
        high_scale[...] = jnp.zeros_like(high_scale)

    loads[0].wait()
    for n in range(25):
        for r in range(R):
            for g in range(planes // SUB):
                x = jac[n, pl.ds(g * SUB, SUB), pl.ds(r * LANES, LANES)].astype(jnp.float32)
                jpack[pl.ds(g * SUB * pitch + r * 25 + n, SUB, stride=pitch), :] = x
    for p in range(planes):
        jsend[p, :, :] = jpack[pl.ds(p * pitch, rows), :].astype(jnp.bfloat16)

    def fill_rims(sweep, field, first, last):
        for c in range(10):
            rim_send[sweep, 0, pl.ds(c, 1), :] = field[c, pl.ds(last, 1), :]
            rim_send[sweep, 1, pl.ds(c, 1), :] = field[c, pl.ds(first, 1), :]

    def rim_copies(sweep):
        return [
            pltpu.make_async_remote_copy(
                src_ref=rim_send.at[sweep, k],
                dst_ref=rim_recv.at[sweep, k],
                send_sem=r_s.at[sweep, k],
                recv_sem=r_r.at[sweep, k],
                device_id={"passage": peer},
                device_id_type=MESH,
            )
            for k, peer in ((0, up_p), (1, down_p))
        ]

    def halo_copies(h_s, h_r, sweep, src, low, high):
        up = pltpu.make_async_remote_copy(
            src_ref=src, dst_ref=low, send_sem=h_s.at[sweep, 0], recv_sem=h_r.at[sweep, 0],
            device_id={"brick": lax.rem(me + 1, B)}, device_id_type=MESH,
        )
        down = pltpu.make_async_remote_copy(
            src_ref=src, dst_ref=high, send_sem=h_s.at[sweep, 1], recv_sem=h_r.at[sweep, 1],
            device_id={"brick": lax.rem(me + B - 1, B)}, device_id_type=MESH,
        )
        return up, down

    def halo_start(up, down):
        @pl.when(me < B - 1)
        def _():
            up.start()

        @pl.when(me > 0)
        def _():
            down.start()

    def halo_recv(up, down):
        @pl.when(me > 0)
        def _():
            up.wait_recv()

        @pl.when(me < B - 1)
        def _():
            down.wait_recv()

    def halo_sent(up, down):
        @pl.when(me < B - 1)
        def _():
            up.wait_send()

        @pl.when(me > 0)
        def _():
            down.wait_send()

    loads[1].wait()
    fill_rims(0, pad0, SUB, SUB + NJ - 1)
    for c in range(10):
        q = jnp.round(pad0[c, pl.ds(SUB, NJ), :] * (CODE / BOUND))
        code0[c, :, :] = q.astype(jnp.int32).astype(jnp.int16)
    loads[2].wait()
    loads[3].wait()
    faces = owner.shape[1]
    ids[...] = jnp.full((SUB, LANES), -1, jnp.int32)
    ids[0:1, pl.ds(0, faces)] = owner[...] * NODE_DEV + slot[...]
    idbuf[pl.ds(me, 1), :, :] = ids[...].reshape(1, SUB, LANES)

    j_copies, id_copies, val_copies = [], [], []
    for k, d in enumerate(others):
        peer = lax.rem(me + d, B)
        j_copies.append(pltpu.make_async_remote_copy(
            src_ref=jsend.at[peer], dst_ref=jrecv.at[me], send_sem=j_s.at[k], recv_sem=j_r.at[k],
            device_id={"brick": peer}, device_id_type=MESH))
        id_copies.append(pltpu.make_async_remote_copy(
            src_ref=ids, dst_ref=idbuf.at[me], send_sem=i_s.at[k], recv_sem=i_r.at[k],
            device_id={"brick": peer}, device_id_type=MESH))
        val_copies.append(pltpu.make_async_remote_copy(
            src_ref=valbuf.at[me], dst_ref=valbuf.at[me], send_sem=v_s.at[k], recv_sem=v_r.at[k],
            device_id={"brick": peer}, device_id_type=MESH))
    rims0, rims1 = rim_copies(0), rim_copies(1)
    halo0 = halo_copies(h_s, h_r, 0, code0, low0, high0)
    halo1 = halo_copies(h_s, h_r, 1, code1, low1, high1)
    scales = halo_copies(c_s, c_r, 0, scale1, low_scale, high_scale)

    pl.semaphore_wait(barrier, greeted)
    for copy in j_copies:
        copy.start()
    for copy in rims0:
        copy.start()
    halo_start(*halo0)
    for copy in id_copies:
        copy.start()

    jrecv[pl.ds(me, 1), :, :] = jsend[pl.ds(me, 1), :, :]
    for load in loads[4:]:
        load.wait()
    normals[...] = jnp.zeros_like(normals)
    for d in range(3):
        for k in (d, 3 + d):
            normals[pl.ds(k, 1), pl.ds(0, faces)] = normals_v[d, :, :]

    lane = lax.broadcasted_iota(jnp.int32, (SUB, NK), 1)

    def place_rims(sweep, pad):
        for k, (edge, turn, row) in enumerate(
            ((0, -phase_angle, SUB - 1), (passes - 1, phase_angle, SUB + NJ))
        ):
            rim = rim_recv[sweep, k, :, :]
            re, im = rim[0:5], rim[5:10]
            at_edge = mp == edge
            cosine = jnp.where(at_edge, math.cos(turn), 1.0).astype(jnp.float32)
            sine = jnp.where(at_edge, math.sin(turn), 0.0).astype(jnp.float32)
            re, im = re * cosine - im * sine, re * sine + im * cosine
            for c in range(5):
                pad[c, pl.ds(row, 1), :] = re[c : c + 1]
                pad[5 + c, pl.ds(row, 1), :] = im[c : c + 1]

    def advance(pad, low, high, out, shift):
        for t in range(NJ // SUB):
            at = pl.ds(t * SUB, SUB)
            om, ds_, ps = freq[at, :], diss[at, :], pstep[at, :]
            us, lows, highs = [], [], []
            for c in range(10):
                us.append(pad[c, pl.ds(SUB + t * SUB, SUB), :])
                lows.append(low[c, at, :])
                highs.append(high[c, at, :])
            diff = [0.5 * (h - l) for h, l in zip(highs, lows)]
            conv = [None] * 10
            for n in range(5):
                for m in range(5):
                    tile = jflat[pl.ds(t * SUB * 25 + n * 5 + m, SUB, stride=25), :]
                    for part in (0, 5):
                        term = tile * diff[part + n]
                        conv[part + m] = term if conv[part + m] is None else conv[part + m] + term
            for c in range(10):
                u = us[c]
                beside = highs[c] + lows[c]
                beside = beside + pad[c, pl.ds(SUB + t * SUB + 1, SUB), :]
                beside = beside + pad[c, pl.ds(SUB + t * SUB - 1, SUB), :]
                beside = beside + jnp.where(lane == NK - 1, 0.0, pltpu.roll(u, NK - 1, 1))
                beside = beside + jnp.where(lane == 0, 0.0, pltpu.roll(u, 1, 1))
                spin = om * us[c + 5] if c < 5 else -(om * us[c - 5])
                resid = conv[c] + spin + ds_ * (6.0 * u - beside) - source[c, at, :]
                out[c, pl.ds(shift + t * SUB, SUB), :] = u - ps * resid

    for copy in rims0:
        copy.wait_recv()
    place_rims(0, pad0)
    halo_recv(*halo0)
    for code, field in ((low0, low), (high0, high)):
        for c in range(10):
            field[c, :, :] = code[c, :, :].astype(jnp.int32).astype(jnp.float32) * (BOUND / CODE)
    for copy in j_copies:
        copy.wait_recv()
    for s in range(B):
        jflat[pl.ds(s * rows, rows), :] = jrecv[s, :, :].astype(jnp.float32)

    advance(pad0, low, high, pad1, SUB)
    fill_rims(1, pad1, SUB, SUB + NJ - 1)
    for copy in rims1:
        copy.start()
    for c in range(10):
        x = pad1[c, pl.ds(SUB, NJ), :]
        top = jnp.maximum(jnp.max(jnp.abs(x), axis=0, keepdims=True), 1e-30)
        scale1[pl.ds(c, 1), :] = top * (1.0 / CODE)
        code1[c, :, :] = jnp.round(x * (CODE / top)).astype(jnp.int32).astype(jnp.int16)
    halo_start(*scales)
    halo_start(*halo1)
    for copy in rims1:
        copy.wait_recv()
    place_rims(1, pad1)
    halo_recv(*scales)
    halo_recv(*halo1)
    for code, scale, field in ((low1, low_scale, low), (high1, high_scale, high)):
        for c in range(10):
            f = code[c, :, :].astype(jnp.int32).astype(jnp.float32)
            field[c, :, :] = f * scale[pl.ds(c, 1), :]
    advance(pad1, low, high, adj, 0)
    store = pltpu.make_async_copy(adj, adj_h, o_s)

    lanes = lax.broadcasted_iota(jnp.int32, (NJ, NK), 1)
    wall = jnp.zeros((NJ, NK), jnp.float32)
    for k, c in enumerate((1, 2, 3, 6, 7, 8)):
        column = adj[c, :, :]
        if k:
            column = pltpu.roll(column, k, 1)
        wall = jnp.where(lanes == k, column, wall)
    if NJ < LANES:
        wall = jnp.concatenate([wall, jnp.zeros((LANES - NJ, NK), jnp.float32)], axis=0)
    values = wall.T[0:SUB] * normals[...]
    valbuf[pl.ds(me, 1), :, :] = values.reshape(1, SUB, LANES)
    for copy in val_copies:
        copy.start()
    store.start()

    for copy in id_copies:
        copy.wait_recv()
    for copy in val_copies:
        copy.wait_recv()
    node = lax.broadcasted_iota(jnp.int32, (NODE_DEV, LANES), 0) + me * NODE_DEV
    total = jnp.zeros((3 * SUB, NODE_DEV), jnp.float32)
    for s in range(B):
        hit = jnp.where(idbuf[s, 0:1, :] == node, 1.0, 0.0).astype(jnp.bfloat16)
        v = valbuf[s, :, :]
        a = v.astype(jnp.bfloat16).astype(jnp.float32)
        rest = v - a
        b = rest.astype(jnp.bfloat16).astype(jnp.float32)
        parts = jnp.concatenate([a, b, rest - b], axis=0).astype(jnp.bfloat16)
        total = total + lax.dot_general(
            parts, hit, (((1,), (1,)), ((), ())), preferred_element_type=jnp.float32
        )
    summed = total[0:SUB] + total[SUB : 2 * SUB] + total[2 * SUB :]
    sens[...] = summed[0:6].reshape(6, 1, NODE_DEV)
    store.wait()

    for copy in j_copies + id_copies + val_copies + rims0 + rims1:
        copy.wait_send()
    halo_sent(*halo0)
    halo_sent(*halo1)
    halo_sent(*scales)


def hand_over(adj, sens, adj_out, sens_out, adj_v, sens_v, in_s, out_s):
    parts = [(sens, sens_v, sens_out)]
    for k in range(5):
        at = pl.ds(2 * k, 2)
        parts.append((adj.at[at], adj_v.at[at], adj_out.at[at]))
    ins = [pltpu.make_async_copy(a, v, in_s.at[k]) for k, (a, v, _) in enumerate(parts)]
    outs = [pltpu.make_async_copy(v, o, out_s.at[k]) for k, (_, v, o) in enumerate(parts)]
    for copy in ins:
        copy.start()
    for arrive, leave in zip(ins, outs):
        arrive.wait()
        leave.start()
    for copy in outs:
        copy.wait()


def body(B, passes, jac_blocks, psi_start, source, pseudo_step, dissipation, freq_volume,
         normals, face_owner, face_slot):
    _, _, planes_all, cells = jac_blocks.shape
    NJ, NK = psi_start.shape[3:]
    phase_angle = 2.0 * math.pi * ND * passes / BLADES
    R = cells // LANES
    rows = 25 * R
    pitch = -(-rows // SUB) * SUB
    faces = face_slot.shape[1]
    f32 = jnp.float32
    i16 = jnp.int16
    field, plane = (10, NJ, NK), (NJ, NK)
    hbm = pl.BlockSpec(memory_space=pl.ANY)
    vm = pl.BlockSpec(memory_space=pltpu.VMEM)
    dma = pltpu.SemaphoreType.DMA
    adj, sens = pl.pallas_call(
        functools.partial(kernel, B, passes, phase_angle),
        out_shape=(
            jax.ShapeDtypeStruct(field, f32),
            jax.ShapeDtypeStruct((6, 1, NODE_DEV), f32),
        ),
        in_specs=[hbm] * 9,
        out_specs=(hbm, vm),
        scratch_shapes=[
            pltpu.VMEM((25, planes_all, cells), jnp.bfloat16),
            pltpu.VMEM(field, f32),
            pltpu.VMEM(plane, f32),
            pltpu.VMEM(plane, f32),
            pltpu.VMEM(plane, f32),
            pltpu.VMEM((3, 1, faces), f32),
            pltpu.VMEM((1, faces), jnp.int32),
            pltpu.VMEM((1, faces), jnp.int32),
            pltpu.VMEM(field, f32),
            pltpu.VMEM((SUB, LANES), f32),
            pltpu.VMEM((SUB, LANES), jnp.int32),
            pltpu.VMEM((planes_all * pitch, LANES), f32),
            pltpu.VMEM((planes_all, rows, LANES), jnp.bfloat16),
            pltpu.VMEM((planes_all, rows, LANES), jnp.bfloat16),
            pltpu.VMEM((B * rows, LANES), f32),
            pltpu.VMEM((10, NJ + 2 * SUB, NK), f32),
            pltpu.VMEM((10, NJ + 2 * SUB, NK), f32),
            pltpu.VMEM(field, f32),
            pltpu.VMEM(field, f32),
            pltpu.VMEM(field, i16),
            pltpu.VMEM(field, i16),
            pltpu.VMEM(field, i16),
            pltpu.VMEM(field, i16),
            pltpu.VMEM(field, i16),
            pltpu.VMEM(field, i16),
            pltpu.VMEM((2 * SUB, NK), f32),
            pltpu.VMEM((2 * SUB, NK), f32),
            pltpu.VMEM((2 * SUB, NK), f32),
            pltpu.VMEM((2, 2, 2 * SUB, NK), f32),
            pltpu.VMEM((2, 2, 2 * SUB, NK), f32),
            pltpu.VMEM((B, SUB, LANES), jnp.int32),
            pltpu.VMEM((B, SUB, LANES), f32),
            dma((9,)), dma,
            dma((B,)), dma((B,)),
            dma((2, 2)), dma((2, 2)),
            dma((1, 2)), dma((1, 2)),
            dma((2, 2)), dma((2, 2)),
            dma((B,)), dma((B,)),
            dma((B,)), dma((B,)),
        ],
        compiler_params=pltpu.CompilerParams(collective_id=0, has_side_effects=True),
        name="flutter",
    )(jac_blocks[0], psi_start[0, :, 0], source[0, :, 0], pseudo_step[0, 0], dissipation[0, 0],
      freq_volume[0, 0], normals[0], face_owner[:, :, 0], face_slot)
    adj, sens = pl.pallas_call(
        hand_over,
        out_shape=(
            jax.ShapeDtypeStruct(field, f32),
            jax.ShapeDtypeStruct((6, 1, NODE_DEV), f32),
        ),
        in_specs=[hbm, hbm],
        out_specs=(hbm, hbm),
        scratch_shapes=[
            pltpu.VMEM(field, f32),
            pltpu.VMEM((6, 1, NODE_DEV), f32),
            dma((6,)), dma((6,)),
        ],
        name="hand_over",
    )(adj, sens)
    return adj[None, :, None], jnp.transpose(sens, (1, 0, 2))


def solution(mesh):
    placed = (
        P("passage", None, None, "brick"),
        P("passage", None, "brick", None, None),
        P("passage", None, "brick", None, None),
        P("passage", "brick", None, None),
        P("passage", "brick", None, None),
        P("passage", "brick", None, None),
        P("passage", None, "brick", None),
        P("passage", "brick", None),
        P("passage", "brick"),
    )
    return jax.shard_map(
        functools.partial(body, mesh.shape["brick"], mesh.shape["passage"]),
        mesh=mesh,
        in_specs=placed,
        out_specs=(P("passage", None, "brick", None, None), P("passage", None, "brick")),
        check_vma=False,
    )
```

```python
import functools
import math

import jax
import jax.numpy as jnp
from jax import lax
from jax.experimental import pallas as pl
from jax.experimental.pallas import tpu as pltpu
from jax.sharding import PartitionSpec as P

NODE_DEV = 256
SWEEPS = 2
ND = 1
BLADES = 36
LANES = 128
SUB = 8
CODE = 32767.0
BOUND = 6.0
MESH = pl.DeviceIdType.MESH


def kernel(
    B, passes, phase_angle,
    jac_h, psi_h, source_h, pstep_h, diss_h, freq_h, normals_h, owner_h, slot_h,
    adj_h, sens,
    jac, source, pstep, diss, freq, normals_v, owner, slot, adj, normals, ids,
    jpack, jsend, jrecv, jflat, pad0, pad1, low, high,
    code0, low0, high0, code1, low1, high1, scale1, low_scale, high_scale,
    rim_send, rim_recv, idbuf, valbuf, hits, turned, wall_send, low_wall, high_wall, rim_wall,
    l_s, o_s, j_s, j_r, h_s, h_r, c_s, c_r, w_s, w_r, r_s, r_r, i_s, i_r, v_s, v_r,
):
    me = lax.axis_index("brick")
    mp = lax.axis_index("passage")
    NJ, NK = source.shape[1], source.shape[2]
    R = jac.shape[2] // LANES
    planes = jac.shape[1]
    rows = 25 * R
    pitch = jpack.shape[0] // planes
    others = range(1, B)
    up_p = lax.rem(mp + 1, passes)
    down_p = lax.rem(mp + passes - 1, passes)

    barrier = pltpu.get_barrier_semaphore()
    for d in others:
        pl.semaphore_signal(
            barrier, inc=1, device_id={"brick": lax.rem(me + d, B)}, device_id_type=MESH
        )
    pl.semaphore_signal(barrier, inc=1, device_id={"passage": up_p}, device_id_type=MESH)
    greeted = B
    if passes > 2:
        pl.semaphore_signal(barrier, inc=1, device_id={"passage": down_p}, device_id_type=MESH)
        greeted += 1

    psi = pad0.at[:, pl.ds(SUB, NJ), :]
    loads = [
        pltpu.make_async_copy(src, dst, l_s.at[k])
        for k, (src, dst) in enumerate((
            (jac_h, jac), (psi_h, psi), (owner_h, owner), (slot_h, slot), (normals_h, normals_v),
            (source_h, source), (pstep_h, pstep), (diss_h, diss), (freq_h, freq),
        ))
    ]
    for load in loads:
        load.start()

    @pl.when(me == 0)
    def _():
        low0[...] = jnp.zeros_like(low0)
        low1[...] = jnp.zeros_like(low1)
        low_scale[...] = jnp.zeros_like(low_scale)
        low_wall[...] = jnp.zeros_like(low_wall)

    @pl.when(me == B - 1)
    def _():
        high0[...] = jnp.zeros_like(high0)
        high1[...] = jnp.zeros_like(high1)
        high_scale[...] = jnp.zeros_like(high_scale)
        high_wall[...] = jnp.zeros_like(high_wall)

    loads[0].wait()
    for n in range(25):
        for r in range(R):
            for g in range(planes // SUB):
                x = jac[n, pl.ds(g * SUB, SUB), pl.ds(r * LANES, LANES)].astype(jnp.float32)
                jpack[pl.ds(g * SUB * pitch + r * 25 + n, SUB, stride=pitch), :] = x
    for p in range(planes):
        jsend[p, :, :] = jpack[pl.ds(p * pitch, rows), :].astype(jnp.bfloat16)

    def fill_rims(sweep, field, first, last):
        for c in range(10):
            rim_send[sweep, 0, pl.ds(c, 1), :] = field[c, pl.ds(last, 1), :]
            rim_send[sweep, 1, pl.ds(c, 1), :] = field[c, pl.ds(first, 1), :]

    def rim_copies(sweep):
        return [
            pltpu.make_async_remote_copy(
                src_ref=rim_send.at[sweep, k],
                dst_ref=rim_recv.at[sweep, k],
                send_sem=r_s.at[sweep, k],
                recv_sem=r_r.at[sweep, k],
                device_id={"passage": peer},
                device_id_type=MESH,
            )
            for k, peer in ((0, up_p), (1, down_p))
        ]

    def halo_copies(h_s, h_r, sweep, src, low, high):
        up = pltpu.make_async_remote_copy(
            src_ref=src, dst_ref=low, send_sem=h_s.at[sweep, 0], recv_sem=h_r.at[sweep, 0],
            device_id={"brick": lax.rem(me + 1, B)}, device_id_type=MESH,
        )
        down = pltpu.make_async_remote_copy(
            src_ref=src, dst_ref=high, send_sem=h_s.at[sweep, 1], recv_sem=h_r.at[sweep, 1],
            device_id={"brick": lax.rem(me + B - 1, B)}, device_id_type=MESH,
        )
        return up, down

    def halo_start(up, down):
        @pl.when(me < B - 1)
        def _():
            up.start()

        @pl.when(me > 0)
        def _():
            down.start()

    def halo_recv(up, down):
        @pl.when(me > 0)
        def _():
            up.wait_recv()

        @pl.when(me < B - 1)
        def _():
            down.wait_recv()

    def halo_sent(up, down):
        @pl.when(me < B - 1)
        def _():
            up.wait_send()

        @pl.when(me > 0)
        def _():
            down.wait_send()

    loads[1].wait()
    fill_rims(0, pad0, SUB, SUB + NJ - 1)
    for c in range(10):
        q = jnp.round(pad0[c, pl.ds(SUB, NJ), :] * (CODE / BOUND))
        code0[c, :, :] = q.astype(jnp.int32).astype(jnp.int16)
    loads[2].wait()
    loads[3].wait()
    faces = owner.shape[1]
    ids[...] = jnp.full((SUB, LANES), -1, jnp.int32)
    ids[0:1, pl.ds(0, faces)] = owner[...] * NODE_DEV + slot[...]
    idbuf[pl.ds(me, 1), :, :] = ids[...].reshape(1, SUB, LANES)

    j_copies, id_copies, val_copies = [], [], []
    for k, d in enumerate(others):
        peer = lax.rem(me + d, B)
        j_copies.append(pltpu.make_async_remote_copy(
            src_ref=jsend.at[peer], dst_ref=jrecv.at[me], send_sem=j_s.at[k], recv_sem=j_r.at[k],
            device_id={"brick": peer}, device_id_type=MESH))
        id_copies.append(pltpu.make_async_remote_copy(
            src_ref=ids, dst_ref=idbuf.at[me], send_sem=i_s.at[k], recv_sem=i_r.at[k],
            device_id={"brick": peer}, device_id_type=MESH))
        val_copies.append(pltpu.make_async_remote_copy(
            src_ref=valbuf.at[me], dst_ref=valbuf.at[me], send_sem=v_s.at[k], recv_sem=v_r.at[k],
            device_id={"brick": peer}, device_id_type=MESH))
    rims0, rims1 = rim_copies(0), rim_copies(1)
    halo0 = halo_copies(h_s, h_r, 0, code0, low0, high0)
    halo1 = halo_copies(h_s, h_r, 1, code1, low1, high1)
    walls = halo_copies(w_s, w_r, 0, wall_send, low_wall, high_wall)
    scales = halo_copies(c_s, c_r, 0, scale1, low_scale, high_scale)

    pl.semaphore_wait(barrier, greeted)
    for copy in id_copies:
        copy.start()
    for copy in j_copies:
        copy.start()
    for copy in rims0:
        copy.start()
    halo_start(*halo0)

    jrecv[pl.ds(me, 1), :, :] = jsend[pl.ds(me, 1), :, :]
    for load in loads[4:]:
        load.wait()
    normals[...] = jnp.zeros_like(normals)
    for d in range(3):
        for k in (d, 3 + d):
            normals[pl.ds(k, 1), pl.ds(0, faces)] = normals_v[d, :, :]

    lane = lax.broadcasted_iota(jnp.int32, (SUB, NK), 1)

    def place_rims(sweep, pad):
        for k, (edge, turn, row) in enumerate(
            ((0, -phase_angle, SUB - 1), (passes - 1, phase_angle, SUB + NJ))
        ):
            rim = rim_recv[sweep, k, :, :]
            re, im = rim[0:5], rim[5:10]
            at_edge = mp == edge
            cosine = jnp.where(at_edge, math.cos(turn), 1.0).astype(jnp.float32)
            sine = jnp.where(at_edge, math.sin(turn), 0.0).astype(jnp.float32)
            re, im = re * cosine - im * sine, re * sine + im * cosine
            if sweep == SWEEPS - 1:
                rim_wall[k, 0:5, :] = re
                rim_wall[k, SUB : SUB + 5, :] = im
            for c in range(5):
                pad[c, pl.ds(row, 1), :] = re[c : c + 1]
                pad[5 + c, pl.ds(row, 1), :] = im[c : c + 1]

    def advance(pad, low, high, out, shift):
        for t in range(NJ // SUB):
            at = pl.ds(t * SUB, SUB)
            om, ds_, ps = freq[at, :], diss[at, :], pstep[at, :]
            us, lows, highs = [], [], []
            for c in range(10):
                us.append(pad[c, pl.ds(SUB + t * SUB, SUB), :])
                lows.append(low[c, at, :])
                highs.append(high[c, at, :])
            diff = [0.5 * (h - l) for h, l in zip(highs, lows)]
            conv = [None] * 10
            for n in range(5):
                for m in range(5):
                    tile = jflat[pl.ds(t * SUB * 25 + n * 5 + m, SUB, stride=25), :]
                    for part in (0, 5):
                        term = tile * diff[part + n]
                        conv[part + m] = term if conv[part + m] is None else conv[part + m] + term
            for c in range(10):
                u = us[c]
                beside = highs[c] + lows[c]
                beside = beside + pad[c, pl.ds(SUB + t * SUB + 1, SUB), :]
                beside = beside + pad[c, pl.ds(SUB + t * SUB - 1, SUB), :]
                beside = beside + jnp.where(lane == NK - 1, 0.0, pltpu.roll(u, NK - 1, 1))
                beside = beside + jnp.where(lane == 0, 0.0, pltpu.roll(u, 1, 1))
                spin = om * us[c + 5] if c < 5 else -(om * us[c - 5])
                resid = conv[c] + spin + ds_ * (6.0 * u - beside) - source[c, at, :]
                out[c, pl.ds(shift + t * SUB, SUB), :] = u - ps * resid

    lanes = lax.broadcasted_iota(jnp.int32, (NJ, NK), 1)

    def turn_over(slot, pieces):
        packed = jnp.zeros((NJ, NK), jnp.float32)
        for to, column, x in pieces:
            shift = (to - column) % NK
            x = pltpu.roll(x, shift, 1) if shift else x
            packed = jnp.where(lanes == to, x, packed)
        if NJ < LANES:
            packed = jnp.concatenate([packed, jnp.zeros((LANES - NJ, NK), jnp.float32)], axis=0)
        turned[slot, :, :] = packed.T

    turn_over(0, [(0, 0, pstep[...]), (1, 0, diss[...]), (2, 0, freq[...])]
              + [(SUB + c + c // 5 * 3, 0, source[c, :, :]) for c in range(10)])
    for copy in id_copies:
        copy.wait_recv()
    node = lax.broadcasted_iota(jnp.int32, (NODE_DEV, LANES), 0) + me * NODE_DEV
    for s in range(B):
        hits[s, :, :] = jnp.where(idbuf[s, 0:1, :] == node, 1.0, 0.0).astype(jnp.bfloat16)

    for copy in rims0:
        copy.wait_recv()
    place_rims(0, pad0)
    halo_recv(*halo0)
    for code, field in ((low0, low), (high0, high)):
        for c in range(10):
            field[c, :, :] = code[c, :, :].astype(jnp.int32).astype(jnp.float32) * (BOUND / CODE)
    for copy in j_copies:
        copy.wait_recv()
    for s in range(B):
        jflat[pl.ds(s * rows, rows), :] = jrecv[s, :, :].astype(jnp.float32)

    advance(pad0, low, high, pad1, SUB)
    fill_rims(1, pad1, SUB, SUB + NJ - 1)
    for copy in rims1:
        copy.start()
    turn_over(2, [
        (16 * k + c + c // 5 * 3, k, pad1[c, pl.ds(SUB, NJ), :]) for k in range(2) for c in range(10)
    ])
    wall_send[...] = turned[2, 0:16, :]
    halo_start(*walls)
    for c in range(10):
        x = pad1[c, pl.ds(SUB, NJ), :]
        top = jnp.maximum(jnp.max(jnp.abs(x), axis=0, keepdims=True), 1e-30)
        scale1[pl.ds(c, 1), :] = top * (1.0 / CODE)
        code1[c, :, :] = jnp.round(x * (CODE / top)).astype(jnp.int32).astype(jnp.int16)
    halo_start(*scales)
    halo_start(*halo1)
    for copy in rims1:
        copy.wait_recv()
    place_rims(1, pad1)
    turn_over(1, [
        (SUB * n + m, 0, jflat[pl.ds(n * 5 + m, NJ, stride=25), :])
        for n in range(5) for m in range(5)
    ])
    halo_recv(*walls)
    face = lax.broadcasted_iota(jnp.int32, (5, LANES), 1)
    sides = normals[0:3, :]
    valbuf[pl.ds(me, 1), :, :] = jnp.zeros((1, SUB, LANES), jnp.float32)
    for part in range(2):
        at = pl.ds(SUB * part, 5)
        u, lo, hi = turned[2, at, :], low_wall[at, :], high_wall[at, :]
        diff = 0.5 * (hi - lo)
        conv = turned[1, 0:5, :] * diff[0:1]
        for n in range(1, 5):
            conv = conv + turned[1, pl.ds(SUB * n, 5), :] * diff[n : n + 1]
        below = jnp.where(face == 0, rim_wall[0, at, :][:, 0:1], pltpu.roll(u, 1, 1))
        above = jnp.where(face == NJ - 1, rim_wall[1, at, :][:, 0:1], pltpu.roll(u, LANES - 1, 1))
        beside = hi + lo + above + below + turned[2, pl.ds(16 + SUB * part, 5), :]
        spin = turned[0, 2:3, :] * turned[2, pl.ds(SUB * (1 - part), 5), :]
        spin = -spin if part else spin
        resid = conv + spin + turned[0, 1:2, :] * (6.0 * u - beside)
        resid = resid - turned[0, pl.ds(SUB + SUB * part, 5), :]
        fresh = u - turned[0, 0:1, :] * resid
        valbuf[pl.ds(me, 1), pl.ds(3 * part, 3), :] = (fresh[1:4] * sides)[None]
    for copy in val_copies:
        copy.start()

    halo_recv(*scales)
    halo_recv(*halo1)
    for code, scale, field in ((low1, low_scale, low), (high1, high_scale, high)):
        for c in range(10):
            f = code[c, :, :].astype(jnp.int32).astype(jnp.float32)
            field[c, :, :] = f * scale[pl.ds(c, 1), :]
    advance(pad1, low, high, adj, 0)
    store = pltpu.make_async_copy(adj, adj_h, o_s)

    store.start()

    for copy in val_copies:
        copy.wait_recv()
    total = jnp.zeros((3 * SUB, NODE_DEV), jnp.float32)
    for s in range(B):
        v = valbuf[s, :, :]
        a = v.astype(jnp.bfloat16).astype(jnp.float32)
        rest = v - a
        b = rest.astype(jnp.bfloat16).astype(jnp.float32)
        parts = jnp.concatenate([a, b, rest - b], axis=0).astype(jnp.bfloat16)
        total = total + lax.dot_general(
            parts, hits[s, :, :], (((1,), (1,)), ((), ())), preferred_element_type=jnp.float32
        )
    summed = total[0:SUB] + total[SUB : 2 * SUB] + total[2 * SUB :]
    sens[...] = summed[0:6].reshape(6, 1, NODE_DEV)
    store.wait()

    for copy in j_copies + id_copies + val_copies + rims0 + rims1:
        copy.wait_send()
    halo_sent(*halo0)
    halo_sent(*halo1)
    halo_sent(*scales)
    halo_sent(*walls)


def hand_over(adj, sens, adj_out, sens_out, adj_v, sens_v, in_s, out_s):
    parts = [(sens, sens_v, sens_out)]
    for k in range(5):
        at = pl.ds(2 * k, 2)
        parts.append((adj.at[at], adj_v.at[at], adj_out.at[at]))
    ins = [pltpu.make_async_copy(a, v, in_s.at[k]) for k, (a, v, _) in enumerate(parts)]
    outs = [pltpu.make_async_copy(v, o, out_s.at[k]) for k, (_, v, o) in enumerate(parts)]
    for copy in ins:
        copy.start()
    for arrive, leave in zip(ins, outs):
        arrive.wait()
        leave.start()
    for copy in outs:
        copy.wait()


def body(B, passes, jac_blocks, psi_start, source, pseudo_step, dissipation, freq_volume,
         normals, face_owner, face_slot):
    _, _, planes_all, cells = jac_blocks.shape
    NJ, NK = psi_start.shape[3:]
    phase_angle = 2.0 * math.pi * ND * passes / BLADES
    R = cells // LANES
    rows = 25 * R
    pitch = -(-rows // SUB) * SUB
    faces = face_slot.shape[1]
    f32 = jnp.float32
    i16 = jnp.int16
    field, plane = (10, NJ, NK), (NJ, NK)
    hbm = pl.BlockSpec(memory_space=pl.ANY)
    vm = pl.BlockSpec(memory_space=pltpu.VMEM)
    dma = pltpu.SemaphoreType.DMA
    adj, sens = pl.pallas_call(
        functools.partial(kernel, B, passes, phase_angle),
        out_shape=(
            jax.ShapeDtypeStruct(field, f32),
            jax.ShapeDtypeStruct((6, 1, NODE_DEV), f32),
        ),
        in_specs=[hbm] * 9,
        out_specs=(hbm, vm),
        scratch_shapes=[
            pltpu.VMEM((25, planes_all, cells), jnp.bfloat16),
            pltpu.VMEM(field, f32),
            pltpu.VMEM(plane, f32),
            pltpu.VMEM(plane, f32),
            pltpu.VMEM(plane, f32),
            pltpu.VMEM((3, 1, faces), f32),
            pltpu.VMEM((1, faces), jnp.int32),
            pltpu.VMEM((1, faces), jnp.int32),
            pltpu.VMEM(field, f32),
            pltpu.VMEM((SUB, LANES), f32),
            pltpu.VMEM((SUB, LANES), jnp.int32),
            pltpu.VMEM((planes_all * pitch, LANES), f32),
            pltpu.VMEM((planes_all, rows, LANES), jnp.bfloat16),
            pltpu.VMEM((planes_all, rows, LANES), jnp.bfloat16),
            pltpu.VMEM((B * rows, LANES), f32),
            pltpu.VMEM((10, NJ + 2 * SUB, NK), f32),
            pltpu.VMEM((10, NJ + 2 * SUB, NK), f32),
            pltpu.VMEM(field, f32),
            pltpu.VMEM(field, f32),
            pltpu.VMEM(field, i16),
            pltpu.VMEM(field, i16),
            pltpu.VMEM(field, i16),
            pltpu.VMEM(field, i16),
            pltpu.VMEM(field, i16),
            pltpu.VMEM(field, i16),
            pltpu.VMEM((2 * SUB, NK), f32),
            pltpu.VMEM((2 * SUB, NK), f32),
            pltpu.VMEM((2 * SUB, NK), f32),
            pltpu.VMEM((2, 2, 2 * SUB, NK), f32),
            pltpu.VMEM((2, 2, 2 * SUB, NK), f32),
            pltpu.VMEM((B, SUB, LANES), jnp.int32),
            pltpu.VMEM((B, SUB, LANES), f32),
            pltpu.VMEM((B, NODE_DEV, LANES), jnp.bfloat16),
            pltpu.VMEM((3, NK, LANES), f32),
            pltpu.VMEM((2 * SUB, LANES), f32),
            pltpu.VMEM((2 * SUB, LANES), f32),
            pltpu.VMEM((2 * SUB, LANES), f32),
            pltpu.VMEM((2, 2 * SUB, LANES), f32),
            dma((9,)), dma,
            dma((B,)), dma((B,)),
            dma((2, 2)), dma((2, 2)),
            dma((1, 2)), dma((1, 2)),
            dma((1, 2)), dma((1, 2)),
            dma((2, 2)), dma((2, 2)),
            dma((B,)), dma((B,)),
            dma((B,)), dma((B,)),
        ],
        compiler_params=pltpu.CompilerParams(collective_id=0, has_side_effects=True),
        name="flutter",
    )(jac_blocks[0], psi_start[0, :, 0], source[0, :, 0], pseudo_step[0, 0], dissipation[0, 0],
      freq_volume[0, 0], normals[0], face_owner[:, :, 0], face_slot)
    adj, sens = pl.pallas_call(
        hand_over,
        out_shape=(
            jax.ShapeDtypeStruct(field, f32),
            jax.ShapeDtypeStruct((6, 1, NODE_DEV), f32),
        ),
        in_specs=[hbm, hbm],
        out_specs=(hbm, hbm),
        scratch_shapes=[
            pltpu.VMEM(field, f32),
            pltpu.VMEM((6, 1, NODE_DEV), f32),
            dma((6,)), dma((6,)),
        ],
        name="hand_over",
    )(adj, sens)
    return adj[None, :, None], jnp.transpose(sens, (1, 0, 2))


def solution(mesh):
    placed = (
        P("passage", None, None, "brick"),
        P("passage", None, "brick", None, None),
        P("passage", None, "brick", None, None),
        P("passage", "brick", None, None),
        P("passage", "brick", None, None),
        P("passage", "brick", None, None),
        P("passage", None, "brick", None),
        P("passage", "brick", None),
        P("passage", "brick"),
    )
    return jax.shard_map(
        functools.partial(body, mesh.shape["brick"], mesh.shape["passage"]),
        mesh=mesh,
        in_specs=placed,
        out_specs=(P("passage", None, "brick", None, None), P("passage", None, "brick")),
        check_vma=False,
    )
```

```python
import functools
import math

import jax
import jax.numpy as jnp
from jax import lax
from jax.experimental import pallas as pl
from jax.experimental.pallas import tpu as pltpu
from jax.sharding import PartitionSpec as P

NODE_DEV = 256
SWEEPS = 2
ND = 1
BLADES = 36
LANES = 128
SUB = 8
CODE = 32767.0
BOUND = 6.0
MESH = pl.DeviceIdType.MESH


def kernel(
    B, passes, phase_angle,
    jac_h, psi_h, source_h, pstep_h, diss_h, freq_h, normals_h, owner_h, slot_h,
    adj_h, sens,
    jac, source, pstep, diss, freq, normals_v, owner, slot, adj, normals, ids,
    jpack, jsend, jrecv, jflat, pad0, pad1, low, high,
    code0, low0, high0, code1, low1, high1, scale1, low_scale, high_scale,
    rim_send, rim_recv, idbuf, valbuf, hits, turned, wall_send, low_wall, high_wall, rim_wall,
    l_s, o_s, j_s, j_r, h_s, h_r, c_s, c_r, w_s, w_r, r_s, r_r, i_s, i_r, v_s, v_r,
):
    me = lax.axis_index("brick")
    mp = lax.axis_index("passage")
    NJ, NK = source.shape[1], source.shape[2]
    R = jac.shape[2] // LANES
    planes = jac.shape[1]
    rows = 25 * R
    pitch = jpack.shape[0] // planes
    others = range(1, B)
    up_p = lax.rem(mp + 1, passes)
    down_p = lax.rem(mp + passes - 1, passes)

    barrier = pltpu.get_barrier_semaphore()
    for d in others:
        pl.semaphore_signal(
            barrier, inc=1, device_id={"brick": lax.rem(me + d, B)}, device_id_type=MESH
        )
    pl.semaphore_signal(barrier, inc=1, device_id={"passage": up_p}, device_id_type=MESH)
    greeted = B
    if passes > 2:
        pl.semaphore_signal(barrier, inc=1, device_id={"passage": down_p}, device_id_type=MESH)
        greeted += 1

    psi = pad0.at[:, pl.ds(SUB, NJ), :]
    loads = [
        pltpu.make_async_copy(src, dst, l_s.at[k])
        for k, (src, dst) in enumerate((
            (jac_h, jac), (psi_h, psi), (owner_h, owner), (slot_h, slot), (normals_h, normals_v),
            (source_h, source), (pstep_h, pstep), (diss_h, diss), (freq_h, freq),
        ))
    ]
    for load in loads:
        load.start()

    @pl.when(me == 0)
    def _():
        low0[...] = jnp.zeros_like(low0)
        low1[...] = jnp.zeros_like(low1)
        low_scale[...] = jnp.zeros_like(low_scale)
        low_wall[...] = jnp.zeros_like(low_wall)

    @pl.when(me == B - 1)
    def _():
        high0[...] = jnp.zeros_like(high0)
        high1[...] = jnp.zeros_like(high1)
        high_scale[...] = jnp.zeros_like(high_scale)
        high_wall[...] = jnp.zeros_like(high_wall)

    loads[0].wait()
    for n in range(25):
        for r in range(R):
            for g in range(planes // SUB):
                x = jac[n, pl.ds(g * SUB, SUB), pl.ds(r * LANES, LANES)].astype(jnp.float32)
                jpack[pl.ds(g * SUB * pitch + r * 25 + n, SUB, stride=pitch), :] = x
    for p in range(planes):
        jsend[p, :, :] = jpack[pl.ds(p * pitch, rows), :].astype(jnp.bfloat16)

    def fill_rims(sweep, field, first, last):
        for c in range(10):
            rim_send[sweep, 0, pl.ds(c, 1), :] = field[c, pl.ds(last, 1), :]
            rim_send[sweep, 1, pl.ds(c, 1), :] = field[c, pl.ds(first, 1), :]

    def rim_copies(sweep):
        return [
            pltpu.make_async_remote_copy(
                src_ref=rim_send.at[sweep, k],
                dst_ref=rim_recv.at[sweep, k],
                send_sem=r_s.at[sweep, k],
                recv_sem=r_r.at[sweep, k],
                device_id={"passage": peer},
                device_id_type=MESH,
            )
            for k, peer in ((0, up_p), (1, down_p))
        ]

    def halo_copies(h_s, h_r, sweep, src, low, high):
        up = pltpu.make_async_remote_copy(
            src_ref=src, dst_ref=low, send_sem=h_s.at[sweep, 0], recv_sem=h_r.at[sweep, 0],
            device_id={"brick": lax.rem(me + 1, B)}, device_id_type=MESH,
        )
        down = pltpu.make_async_remote_copy(
            src_ref=src, dst_ref=high, send_sem=h_s.at[sweep, 1], recv_sem=h_r.at[sweep, 1],
            device_id={"brick": lax.rem(me + B - 1, B)}, device_id_type=MESH,
        )
        return up, down

    def halo_start(up, down):
        @pl.when(me < B - 1)
        def _():
            up.start()

        @pl.when(me > 0)
        def _():
            down.start()

    def halo_recv(up, down):
        @pl.when(me > 0)
        def _():
            up.wait_recv()

        @pl.when(me < B - 1)
        def _():
            down.wait_recv()

    def halo_sent(up, down):
        @pl.when(me < B - 1)
        def _():
            up.wait_send()

        @pl.when(me > 0)
        def _():
            down.wait_send()

    loads[1].wait()
    fill_rims(0, pad0, SUB, SUB + NJ - 1)
    for c in range(10):
        q = jnp.round(pad0[c, pl.ds(SUB, NJ), :] * (CODE / BOUND))
        code0[c, :, :] = q.astype(jnp.int32).astype(jnp.int16)
    loads[2].wait()
    loads[3].wait()
    faces = owner.shape[1]
    ids[...] = jnp.full((SUB, LANES), -1, jnp.int32)
    ids[0:1, pl.ds(0, faces)] = owner[...] * NODE_DEV + slot[...]
    idbuf[pl.ds(me, 1), :, :] = ids[...].reshape(1, SUB, LANES)

    j_copies, id_copies, val_copies = [], [], []
    for k, d in enumerate(others):
        peer = lax.rem(me + d, B)
        j_copies.append(pltpu.make_async_remote_copy(
            src_ref=jsend.at[peer], dst_ref=jrecv.at[me], send_sem=j_s.at[k], recv_sem=j_r.at[k],
            device_id={"brick": peer}, device_id_type=MESH))
        id_copies.append(pltpu.make_async_remote_copy(
            src_ref=ids, dst_ref=idbuf.at[me], send_sem=i_s.at[k], recv_sem=i_r.at[k],
            device_id={"brick": peer}, device_id_type=MESH))
        val_copies.append(pltpu.make_async_remote_copy(
            src_ref=valbuf.at[me], dst_ref=valbuf.at[me], send_sem=v_s.at[k], recv_sem=v_r.at[k],
            device_id={"brick": peer}, device_id_type=MESH))
    rims0, rims1 = rim_copies(0), rim_copies(1)
    halo0 = halo_copies(h_s, h_r, 0, code0, low0, high0)
    halo1 = halo_copies(h_s, h_r, 1, code1, low1, high1)
    walls = halo_copies(w_s, w_r, 0, wall_send, low_wall, high_wall)
    scales = halo_copies(c_s, c_r, 0, scale1, low_scale, high_scale)

    pl.semaphore_wait(barrier, greeted)
    for copy in id_copies:
        copy.start()
    for copy in j_copies:
        copy.start()
    for copy in rims0:
        copy.start()
    halo_start(*halo0)

    jrecv[pl.ds(me, 1), :, :] = jsend[pl.ds(me, 1), :, :]
    for load in loads[4:]:
        load.wait()
    normals[...] = jnp.zeros_like(normals)
    for d in range(3):
        for k in (d, 3 + d):
            normals[pl.ds(k, 1), pl.ds(0, faces)] = normals_v[d, :, :]

    lane = lax.broadcasted_iota(jnp.int32, (SUB, NK), 1)

    def place_rims(sweep, pad):
        for k, (edge, turn, row) in enumerate(
            ((0, -phase_angle, SUB - 1), (passes - 1, phase_angle, SUB + NJ))
        ):
            rim = rim_recv[sweep, k, :, :]
            re, im = rim[0:5], rim[5:10]
            at_edge = mp == edge
            cosine = jnp.where(at_edge, math.cos(turn), 1.0).astype(jnp.float32)
            sine = jnp.where(at_edge, math.sin(turn), 0.0).astype(jnp.float32)
            re, im = re * cosine - im * sine, re * sine + im * cosine
            if sweep == SWEEPS - 1:
                rim_wall[k, 0:5, :] = re
                rim_wall[k, SUB : SUB + 5, :] = im
            for c in range(5):
                pad[c, pl.ds(row, 1), :] = re[c : c + 1]
                pad[5 + c, pl.ds(row, 1), :] = im[c : c + 1]

    def advance(pad, low, high, out, shift):
        for t in range(NJ // SUB):
            at = pl.ds(t * SUB, SUB)
            om, ds_, ps = freq[at, :], diss[at, :], pstep[at, :]
            us, lows, highs = [], [], []
            for c in range(10):
                us.append(pad[c, pl.ds(SUB + t * SUB, SUB), :])
                lows.append(low[c, at, :])
                highs.append(high[c, at, :])
            diff = [0.5 * (h - l) for h, l in zip(highs, lows)]
            conv = [None] * 10
            for n in range(5):
                for m in range(5):
                    tile = jflat[pl.ds(t * SUB * step + n * 5 + m, SUB, stride=step), :]
                    for part in (0, 5):
                        term = tile * diff[part + n]
                        conv[part + m] = term if conv[part + m] is None else conv[part + m] + term
            for c in range(10):
                u = us[c]
                beside = highs[c] + lows[c]
                beside = beside + pad[c, pl.ds(SUB + t * SUB + 1, SUB), :]
                beside = beside + pad[c, pl.ds(SUB + t * SUB - 1, SUB), :]
                beside = beside + jnp.where(lane == NK - 1, 0.0, pltpu.roll(u, NK - 1, 1))
                beside = beside + jnp.where(lane == 0, 0.0, pltpu.roll(u, 1, 1))
                spin = om * us[c + 5] if c < 5 else -(om * us[c - 5])
                resid = conv[c] + spin + ds_ * (6.0 * u - beside) - source[c, at, :]
                out[c, pl.ds(shift + t * SUB, SUB), :] = u - ps * resid

    lanes = lax.broadcasted_iota(jnp.int32, (NJ, NK), 1)

    def turn_over(slot, pieces):
        packed = jnp.zeros((NJ, NK), jnp.float32)
        for to, column, x in pieces:
            shift = (to - column) % NK
            x = pltpu.roll(x, shift, 1) if shift else x
            packed = jnp.where(lanes == to, x, packed)
        if NJ < LANES:
            packed = jnp.concatenate([packed, jnp.zeros((LANES - NJ, NK), jnp.float32)], axis=0)
        turned[slot, :, :] = packed.T

    turn_over(0, [(0, 0, pstep[...]), (1, 0, diss[...]), (2, 0, freq[...])]
              + [(SUB + c + c // 5 * 3, 0, source[c, :, :]) for c in range(10)])
    for copy in id_copies:
        copy.wait_recv()
    node = lax.broadcasted_iota(jnp.int32, (NODE_DEV, LANES), 0) + me * NODE_DEV
    for s in range(B):
        hits[s, :, :] = jnp.where(idbuf[s, 0:1, :] == node, 1.0, 0.0).astype(jnp.bfloat16)

    step = jflat.shape[0] // NJ

    def unpack(s):
        x = jrecv[pl.ds(s, 1), :, :].reshape(rows, LANES).astype(jnp.float32)
        base = pl.multiple_of(s * (R * step), SUB)
        for r in range(R):
            jflat[pl.ds(base + r * step, 25), :] = x[r * 25 : r * 25 + 25]

    unpack(me)
    for d, copy in zip(others, j_copies):
        copy.wait_recv()
        unpack(lax.rem(me + B - d, B))

    for copy in rims0:
        copy.wait_recv()
    place_rims(0, pad0)
    halo_recv(*halo0)
    for code, field in ((low0, low), (high0, high)):
        for c in range(10):
            field[c, :, :] = code[c, :, :].astype(jnp.int32).astype(jnp.float32) * (BOUND / CODE)
    advance(pad0, low, high, pad1, SUB)
    fill_rims(1, pad1, SUB, SUB + NJ - 1)
    for copy in rims1:
        copy.start()
    turn_over(2, [
        (16 * k + c + c // 5 * 3, k, pad1[c, pl.ds(SUB, NJ), :]) for k in range(2) for c in range(10)
    ])
    wall_send[...] = turned[2, 0:16, :]
    halo_start(*walls)
    for c in range(10):
        x = pad1[c, pl.ds(SUB, NJ), :]
        top = jnp.maximum(jnp.max(jnp.abs(x), axis=0, keepdims=True), 1e-30)
        scale1[pl.ds(c, 1), :] = top * (1.0 / CODE)
        code1[c, :, :] = jnp.round(x * (CODE / top)).astype(jnp.int32).astype(jnp.int16)
    for copy in rims1:
        copy.wait_recv()
    place_rims(1, pad1)
    turn_over(1, [
        (SUB * n + m, 0, jflat[pl.ds(n * 5 + m, NJ, stride=step), :])
        for n in range(5) for m in range(5)
    ])
    halo_recv(*walls)
    face = lax.broadcasted_iota(jnp.int32, (5, LANES), 1)
    sides = normals[0:3, :]
    valbuf[pl.ds(me, 1), :, :] = jnp.zeros((1, SUB, LANES), jnp.float32)
    for part in range(2):
        at = pl.ds(SUB * part, 5)
        u, lo, hi = turned[2, at, :], low_wall[at, :], high_wall[at, :]
        diff = 0.5 * (hi - lo)
        conv = turned[1, 0:5, :] * diff[0:1]
        for n in range(1, 5):
            conv = conv + turned[1, pl.ds(SUB * n, 5), :] * diff[n : n + 1]
        below = jnp.where(face == 0, rim_wall[0, at, :][:, 0:1], pltpu.roll(u, 1, 1))
        above = jnp.where(face == NJ - 1, rim_wall[1, at, :][:, 0:1], pltpu.roll(u, LANES - 1, 1))
        beside = hi + lo + above + below + turned[2, pl.ds(16 + SUB * part, 5), :]
        spin = turned[0, 2:3, :] * turned[2, pl.ds(SUB * (1 - part), 5), :]
        spin = -spin if part else spin
        resid = conv + spin + turned[0, 1:2, :] * (6.0 * u - beside)
        resid = resid - turned[0, pl.ds(SUB + SUB * part, 5), :]
        fresh = u - turned[0, 0:1, :] * resid
        valbuf[pl.ds(me, 1), pl.ds(3 * part, 3), :] = (fresh[1:4] * sides)[None]
    for copy in val_copies:
        copy.start()
    halo_start(*scales)
    halo_start(*halo1)

    halo_recv(*scales)
    halo_recv(*halo1)
    for code, scale, field in ((low1, low_scale, low), (high1, high_scale, high)):
        for c in range(10):
            f = code[c, :, :].astype(jnp.int32).astype(jnp.float32)
            field[c, :, :] = f * scale[pl.ds(c, 1), :]
    advance(pad1, low, high, adj, 0)
    store = pltpu.make_async_copy(adj, adj_h, o_s)

    store.start()

    for copy in val_copies:
        copy.wait_recv()
    total = jnp.zeros((3 * SUB, NODE_DEV), jnp.float32)
    for s in range(B):
        v = valbuf[s, :, :]
        a = v.astype(jnp.bfloat16).astype(jnp.float32)
        rest = v - a
        b = rest.astype(jnp.bfloat16).astype(jnp.float32)
        parts = jnp.concatenate([a, b, rest - b], axis=0).astype(jnp.bfloat16)
        total = total + lax.dot_general(
            parts, hits[s, :, :], (((1,), (1,)), ((), ())), preferred_element_type=jnp.float32
        )
    summed = total[0:SUB] + total[SUB : 2 * SUB] + total[2 * SUB :]
    sens[...] = summed[0:6].reshape(6, 1, NODE_DEV)
    store.wait()

    for copy in j_copies + id_copies + val_copies + rims0 + rims1:
        copy.wait_send()
    halo_sent(*halo0)
    halo_sent(*halo1)
    halo_sent(*scales)
    halo_sent(*walls)


def hand_over(adj, sens, adj_out, sens_out, adj_v, sens_v, in_s, out_s):
    parts = [(sens, sens_v, sens_out)]
    for k in range(5):
        at = pl.ds(2 * k, 2)
        parts.append((adj.at[at], adj_v.at[at], adj_out.at[at]))
    ins = [pltpu.make_async_copy(a, v, in_s.at[k]) for k, (a, v, _) in enumerate(parts)]
    outs = [pltpu.make_async_copy(v, o, out_s.at[k]) for k, (_, v, o) in enumerate(parts)]
    for copy in ins:
        copy.start()
    for arrive, leave in zip(ins, outs):
        arrive.wait()
        leave.start()
    for copy in outs:
        copy.wait()


def body(B, passes, jac_blocks, psi_start, source, pseudo_step, dissipation, freq_volume,
         normals, face_owner, face_slot):
    _, _, planes_all, cells = jac_blocks.shape
    NJ, NK = psi_start.shape[3:]
    phase_angle = 2.0 * math.pi * ND * passes / BLADES
    R = cells // LANES
    rows = 25 * R
    pitch = -(-rows // SUB) * SUB
    faces = face_slot.shape[1]
    step = next(k for k in range(25, 33) if R * k % SUB == 0)
    f32 = jnp.float32
    i16 = jnp.int16
    field, plane = (10, NJ, NK), (NJ, NK)
    hbm = pl.BlockSpec(memory_space=pl.ANY)
    vm = pl.BlockSpec(memory_space=pltpu.VMEM)
    dma = pltpu.SemaphoreType.DMA
    adj, sens = pl.pallas_call(
        functools.partial(kernel, B, passes, phase_angle),
        out_shape=(
            jax.ShapeDtypeStruct(field, f32),
            jax.ShapeDtypeStruct((6, 1, NODE_DEV), f32),
        ),
        in_specs=[hbm] * 9,
        out_specs=(hbm, vm),
        scratch_shapes=[
            pltpu.VMEM((25, planes_all, cells), jnp.bfloat16),
            pltpu.VMEM(field, f32),
            pltpu.VMEM(plane, f32),
            pltpu.VMEM(plane, f32),
            pltpu.VMEM(plane, f32),
            pltpu.VMEM((3, 1, faces), f32),
            pltpu.VMEM((1, faces), jnp.int32),
            pltpu.VMEM((1, faces), jnp.int32),
            pltpu.VMEM(field, f32),
            pltpu.VMEM((SUB, LANES), f32),
            pltpu.VMEM((SUB, LANES), jnp.int32),
            pltpu.VMEM((planes_all * pitch, LANES), f32),
            pltpu.VMEM((planes_all, rows, LANES), jnp.bfloat16),
            pltpu.VMEM((planes_all, rows, LANES), jnp.bfloat16),
            pltpu.VMEM((NJ * step, LANES), f32),
            pltpu.VMEM((10, NJ + 2 * SUB, NK), f32),
            pltpu.VMEM((10, NJ + 2 * SUB, NK), f32),
            pltpu.VMEM(field, f32),
            pltpu.VMEM(field, f32),
            pltpu.VMEM(field, i16),
            pltpu.VMEM(field, i16),
            pltpu.VMEM(field, i16),
            pltpu.VMEM(field, i16),
            pltpu.VMEM(field, i16),
            pltpu.VMEM(field, i16),
            pltpu.VMEM((2 * SUB, NK), f32),
            pltpu.VMEM((2 * SUB, NK), f32),
            pltpu.VMEM((2 * SUB, NK), f32),
            pltpu.VMEM((2, 2, 2 * SUB, NK), f32),
            pltpu.VMEM((2, 2, 2 * SUB, NK), f32),
            pltpu.VMEM((B, SUB, LANES), jnp.int32),
            pltpu.VMEM((B, SUB, LANES), f32),
            pltpu.VMEM((B, NODE_DEV, LANES), jnp.bfloat16),
            pltpu.VMEM((3, NK, LANES), f32),
            pltpu.VMEM((2 * SUB, LANES), f32),
            pltpu.VMEM((2 * SUB, LANES), f32),
            pltpu.VMEM((2 * SUB, LANES), f32),
            pltpu.VMEM((2, 2 * SUB, LANES), f32),
            dma((9,)), dma,
            dma((B,)), dma((B,)),
            dma((2, 2)), dma((2, 2)),
            dma((1, 2)), dma((1, 2)),
            dma((1, 2)), dma((1, 2)),
            dma((2, 2)), dma((2, 2)),
            dma((B,)), dma((B,)),
            dma((B,)), dma((B,)),
        ],
        compiler_params=pltpu.CompilerParams(collective_id=0, has_side_effects=True),
        name="flutter",
    )(jac_blocks[0], psi_start[0, :, 0], source[0, :, 0], pseudo_step[0, 0], dissipation[0, 0],
      freq_volume[0, 0], normals[0], face_owner[:, :, 0], face_slot)
    adj, sens = pl.pallas_call(
        hand_over,
        out_shape=(
            jax.ShapeDtypeStruct(field, f32),
            jax.ShapeDtypeStruct((6, 1, NODE_DEV), f32),
        ),
        in_specs=[hbm, hbm],
        out_specs=(hbm, hbm),
        scratch_shapes=[
            pltpu.VMEM(field, f32),
            pltpu.VMEM((6, 1, NODE_DEV), f32),
            dma((6,)), dma((6,)),
        ],
        name="hand_over",
    )(adj, sens)
    return adj[None, :, None], jnp.transpose(sens, (1, 0, 2))


def solution(mesh):
    placed = (
        P("passage", None, None, "brick"),
        P("passage", None, "brick", None, None),
        P("passage", None, "brick", None, None),
        P("passage", "brick", None, None),
        P("passage", "brick", None, None),
        P("passage", "brick", None, None),
        P("passage", None, "brick", None),
        P("passage", "brick", None),
        P("passage", "brick"),
    )
    return jax.shard_map(
        functools.partial(body, mesh.shape["brick"], mesh.shape["passage"]),
        mesh=mesh,
        in_specs=placed,
        out_specs=(P("passage", None, "brick", None, None), P("passage", None, "brick")),
        check_vma=False,
    )
```
